128 devices in a mesh: sec: 2 (over y_lo), dp: 16 (over z, y_hi, core), tensor: 4 (over x).
Axes of the slice: x: 4, y: 4 (y_hi: 2, y_lo: 2; y = y_hi * 2 + y_lo), z: 4, core: 2. Of those that a mesh axis runs over, the one named last changes fastest.
Arguments:
- student_rows: bfloat16 [2, 8192, 5376], P('sec', 'dp'), may hold values from -24 to 24
- teacher_rows: bfloat16 [2, 8192, 5376], P('sec', 'dp'), may hold values from -6 to 6
- norm_gain: float32 [5376], replicated, may hold values from 0.5 to 1.5
- post_gain: float32 [5376], replicated, may hold values from 0.5 to 1.5
- query_weight: bfloat16 [5376, 2048], P(('sec', 'dp'), 'tensor')
- key_weight: bfloat16 [5376, 1024], P(('sec', 'dp'), 'tensor')
- value_weight: bfloat16 [5376, 1024], P(('sec', 'dp'), 'tensor'), may hold values from -0.078125 to 0.078125
- out_weight: bfloat16 [5376, 2048], P(('sec', 'dp'), 'tensor'), may hold values from -0.125 to 0.125
Outputs:
- layer_output: bfloat16 [2, 8192, 5376], P('sec', 'dp', 'tensor')
- query_grad: float32 [5376, 2048], P(('sec', 'dp'), 'tensor')
- output_grad: float32 [5376, 2048], P(('sec', 'dp'), 'tensor')
The draws below stay inside these ranges and needn't reach their ends.
All inputs are finite; a program needn't handle non-finite values.
Results may differ from the reference program's by a relative error of at most 0.025.
The reference program's roundings to bfloat16 on the way count: a program that leaves them out, or rounds other values in their place, can miss the bound.
Values may be sent and summed in bfloat16 or wider, within the bound.
A program may use at most 128 MiB of HBM per device.

```python
import math
import jax
import jax.numpy as jnp
from jax import lax

D = 5376
HEADS = 8
KV_HEADS = 4
HD = 256
W = 1024
TOK_DEV = 512
SEQS = 2
LEN = 8192
TOKENS = 16384
N_DP = 16
N_TENSOR = 4


def shared_normal(key):
    return jnp.clip(jax.random.normal(jax.random.fold_in(key, 101), (D, HEADS * HD), jnp.float32), -3.0, 3.0)


def draw_query_weight(key, part):
    values = shared_normal(key) * D ** (-0.5)
    return values.astype(jnp.bfloat16)


def draw_key_weight(key, part):
    fresh_normal = jnp.clip(jax.random.normal(jax.random.fold_in(key, 102), (D, KV_HEADS * HD), jnp.float32), -3.0, 3.0)
    return (fresh_normal * D ** (-0.5)).astype(jnp.bfloat16)


def draw_student_rows(key, part):
    row_scale = jnp.exp(jax.random.uniform(jax.random.fold_in(key, 201), (SEQS, LEN, 1), jnp.float32, -1.15, 1.15))
    column_scale = jnp.exp(jax.random.uniform(jax.random.fold_in(key, 202), (1, 1, D), jnp.float32, -1.15, 1.15))
    values = jax.random.normal(jax.random.fold_in(key, 203), (SEQS, LEN, D), jnp.float32) * row_scale * column_scale
    return jnp.clip(values, -24.0, 24.0).astype(jnp.bfloat16)


def raised(drawn, key, source, target, parts, factor):
    def block_of(dim):
        return (jnp.arange(drawn.shape[dim]) // (drawn.shape[dim] // parts)).reshape((-1,) + (1,) * (drawn.ndim - 1 - dim))

    first = jax.random.permutation(key, parts)[block_of(target)]
    other_side = (block_of(target) + parts // 2) % parts
    return jnp.where((block_of(source) == first) | (block_of(source) == other_side), factor * drawn, drawn)


def steps_of(stream_key, dims, shards, smallest, largest):
    loudness = 1.0
    for axis_at, blocks in shards:
        draws = jax.random.uniform(jax.random.fold_in(jax.random.fold_in(stream_key, 6), axis_at), (blocks,), jnp.float32, smallest / len(shards), largest / len(shards))
        loudness = loudness * jnp.repeat(jnp.exp(draws), dims[axis_at] // blocks).reshape((-1,) + (1,) * (len(dims) - 1 - axis_at))
    return loudness


def gaussian(stream_key, dims, spread, limit, cuts=(), held_as=jnp.bfloat16):
    values = spread * jax.random.normal(stream_key, dims, jnp.float32)
    if cuts:
        values = values * steps_of(stream_key, dims, cuts, -0.22, 0.18)
    return jnp.clip(values, -limit, limit).astype(held_as)


def gaussian_with(own_key, shape, spread, most, pieces, heavy, kind=jnp.bfloat16):
    values = spread * jax.random.normal(own_key, shape, jnp.float32)
    if pieces:
        values = values * steps_of(own_key, shape, pieces, -0.22, 0.18)
    return jnp.clip(raised(values, jax.random.fold_in(own_key, 3), *heavy), -most, most).astype(kind)


def setup_inputs(seed: int = 0) -> dict:
    splits = jax.random.split(jax.random.key(seed), 9)
    return {
        "student_rows": draw_student_rows(jax.random.fold_in(splits[8], 71), 0),
        "teacher_rows": gaussian_with(splits[1], (SEQS, LEN, D), 1.0, 6.0, ((0, 2), (1, 16)), (1, 2, 16, 2.0)),
        "norm_gain": jnp.clip(1.0 + 0.1 * jax.random.normal(splits[2], (D,), jnp.float32), 0.5, 1.5),
        "post_gain": jnp.clip(1.0 + 0.1 * jax.random.normal(splits[3], (D,), jnp.float32), 0.5, 1.5),
        "query_weight": draw_query_weight(jax.random.fold_in(splits[8], 71), 0),
        "key_weight": draw_key_weight(jax.random.fold_in(splits[8], 71), 0),
        "value_weight": gaussian(splits[6], (D, KV_HEADS * HD), D ** -0.5, 0.078125, ((0, 32), (1, 4))),
        "out_weight": gaussian(splits[7], (D, HEADS * HD), (HEADS * HD) ** -0.5, 0.125, ((0, 32), (1, 4))),
    }


norm_eps = 1e-06
rope_base = 10000.0
masked_score = -1e+30
highest = lax.Precision.HIGHEST

def rotate(values, cos_table, sin_table, sign_value):
    row_count = values.shape[0]
    half_dim = cos_table.shape[1]
    per_head = values.reshape(row_count, -1, 2 * half_dim)
    leading = per_head[:, :, :half_dim]
    trailing = per_head[:, :, half_dim:]
    cosines = cos_table[:, None, :]
    sin_scaled = sign_value * sin_table[:, None, :]
    rotated = jnp.concatenate([leading * cosines - trailing * sin_scaled, trailing * cosines + leading * sin_scaled], axis=2)
    return rotated.reshape(row_count, -1)

def rounded(values):
    return lax.optimization_barrier(values.astype(jnp.bfloat16)).astype(jnp.float32)

def reference(student_rows, teacher_rows, norm_gain, post_gain, query_weight, key_weight, value_weight, out_weight):
    tok_count = TOK_DEV
    blocks_back = (W + tok_count - 1) // tok_count
    key_count = (blocks_back + 1) * tok_count
    group_size = HEADS // KV_HEADS
    score_scale = 1.0 / math.sqrt(HD)
    loss_scale = 2.0 / math.sqrt(TOKENS)
    query_cols = HEADS * HD
    kv_cols = KV_HEADS * HD
    tensor_cols = query_cols // N_TENSOR
    half_dim = HD // 2
    inv_freq = jnp.power(jnp.float32(rope_base), -2.0 * jnp.arange(half_dim, dtype=jnp.float32) / HD)
    targets = jnp.roll(teacher_rows, 1, axis=0)
    positions = jnp.arange(LEN, dtype=jnp.int32).astype(jnp.float32)
    angles = positions[:, None] * inv_freq[None, :]
    cos_full = jnp.cos(angles)
    sin_full = jnp.sin(angles)
    pad_rows = blocks_back * tok_count
    out_weight_f = out_weight.astype(jnp.float32).reshape(D, N_TENSOR, tensor_cols)
    layer_list = []
    query_total = jnp.zeros((D, query_cols), jnp.float32)
    out_total = jnp.zeros((D, query_cols), jnp.float32)
    for seq_index in range(SEQS):
        student_f = student_rows[seq_index].astype(jnp.float32)
        inverse = lax.rsqrt(lax.optimization_barrier(jnp.mean(student_f * student_f, axis=1, keepdims=True)) + norm_eps)
        normed = (student_f * inverse * norm_gain).astype(jnp.bfloat16)
        queries = rotate(jnp.dot(normed, query_weight, preferred_element_type=jnp.float32), cos_full, sin_full, 1.0).astype(jnp.bfloat16)
        key_rows = rotate(jnp.dot(normed, key_weight, preferred_element_type=jnp.float32), cos_full, sin_full, 1.0).astype(jnp.bfloat16)
        value_rows = jnp.dot(normed, value_weight, preferred_element_type=jnp.float32).astype(jnp.bfloat16)
        keys_pad = jnp.concatenate([jnp.zeros((pad_rows, kv_cols), jnp.bfloat16), key_rows], axis=0)
        values_pad = jnp.concatenate([jnp.zeros((pad_rows, kv_cols), jnp.bfloat16), value_rows], axis=0)
        target_seq = targets[seq_index]

        def block_step(totals, block_index):
            query_acc, out_acc = totals
            first_pos = block_index * tok_count

            def take_rows(source):
                return lax.dynamic_slice_in_dim(source, first_pos, tok_count, 0)
            student_blk = take_rows(student_f)
            normed_blk = take_rows(normed)
            query_blk = take_rows(queries)
            cos_blk = take_rows(cos_full)
            sin_blk = take_rows(sin_full)
            target_blk = take_rows(target_seq)
            key_win = lax.dynamic_slice_in_dim(keys_pad, first_pos, key_count, 0)
            value_win = lax.dynamic_slice_in_dim(values_pad, first_pos, key_count, 0)
            query_pos = first_pos + jnp.arange(tok_count, dtype=jnp.int32)
            key_pos = first_pos - pad_rows + jnp.arange(key_count, dtype=jnp.int32)
            allowed = (key_pos[None, :] >= 0) & (key_pos[None, :] <= query_pos[:, None]) & (key_pos[None, :] > query_pos[:, None] - W)
            grouped_q = query_blk.astype(jnp.float32).reshape(tok_count, KV_HEADS, group_size, HD)
            grouped_k = key_win.astype(jnp.float32).reshape(key_count, KV_HEADS, HD)
            grouped_v = value_win.astype(jnp.float32).reshape(key_count, KV_HEADS, HD)
            scores = jnp.einsum('tgad,kgd->gatk', grouped_q, grouped_k, precision=highest) * score_scale
            scores = jnp.where(allowed, scores, masked_score)
            row_peak = lax.optimization_barrier(jnp.max(scores, axis=3, keepdims=True))
            exp_scores = jnp.exp(scores - row_peak)
            attn_probs = exp_scores / lax.optimization_barrier(jnp.sum(exp_scores, axis=3, keepdims=True))
            probs_b = attn_probs.astype(jnp.bfloat16)
            mixed_rows = jnp.einsum('gatk,kgd->tgad', probs_b.astype(jnp.float32), grouped_v, precision=highest).astype(jnp.bfloat16).reshape(tok_count, query_cols)
            partial_value = jnp.einsum('tre,dre->rtd', mixed_rows.astype(jnp.float32).reshape(tok_count, N_TENSOR, tensor_cols), out_weight_f, precision=highest)
            summed = lax.optimization_barrier(jnp.sum(rounded(partial_value), axis=0))
            post_factor = lax.rsqrt(lax.optimization_barrier(jnp.mean(summed * summed, axis=1, keepdims=True)) + norm_eps)
            layer_blk = (student_blk + summed * post_factor * post_gain).astype(jnp.bfloat16)
            loss_grad = loss_scale * (layer_blk.astype(jnp.float32) - target_blk.astype(jnp.float32))
            scaled = post_gain * loss_grad
            along_sum = lax.optimization_barrier(jnp.mean(summed * scaled, axis=1, keepdims=True))
            pre_grad = (post_factor * scaled - summed * post_factor * post_factor * post_factor * along_sum).astype(jnp.bfloat16)
            mixed_grad = jnp.dot(pre_grad, out_weight, preferred_element_type=jnp.float32).astype(jnp.bfloat16)
            grouped_g = mixed_grad.astype(jnp.float32).reshape(tok_count, KV_HEADS, group_size, HD)
            prob_grad = jnp.einsum('tgad,kgd->gatk', grouped_g, grouped_v, precision=highest)
            score_grad = (attn_probs * (prob_grad - lax.optimization_barrier(jnp.sum(attn_probs * prob_grad, axis=3, keepdims=True)))).astype(jnp.bfloat16)
            rotated_grad = jnp.einsum('gatk,kgd->tgad', score_grad.astype(jnp.float32), grouped_k, precision=highest).reshape(tok_count, query_cols) * score_scale
            query_pre = rotate(rotated_grad, cos_blk, sin_blk, -1.0).astype(jnp.bfloat16)
            query_term = jnp.dot(normed_blk.T, query_pre, preferred_element_type=jnp.float32)
            out_term = jnp.dot(pre_grad.T, mixed_rows, preferred_element_type=jnp.float32)
            return ((query_acc + rounded(query_term), out_acc + rounded(out_term)), layer_blk)
        (query_total, out_total), layer_blocks = lax.scan(block_step, (query_total, out_total), jnp.arange(N_DP, dtype=jnp.int32))
        layer_list.append(layer_blocks.reshape(LEN, D))
    return (jnp.stack(layer_list, axis=0), query_total, out_total)
```

```python
import math

import jax
import jax.numpy as jnp
from jax import lax
from jax.experimental import pallas as pl
from jax.experimental.pallas import tpu as pltpu
from jax.sharding import PartitionSpec as P

HEADS = 8
KV_HEADS = 4
HD = 256
W = 1024
MESH = pl.DeviceIdType.MESH
VMEM_CAP = 60 * 1024 * 1024

norm_eps = 1e-06
rope_base = 10000.0
masked_score = -1e30


def where_am_i():
    sec, dp = lax.axis_index("sec"), lax.axis_index("dp")
    z = lax.div(dp, 4)
    y = lax.rem(lax.div(dp, 2), 2) * 2 + sec
    return y, z, lax.rem(dp, 2)


def mod4(v):
    return lax.rem(v + 4, 4)


def device_at(y, z, c):
    return {"sec": lax.rem(y, 2), "dp": z * 4 + lax.div(y, 2) * 2 + c}


def block_at(y, z, c):
    return lax.rem(y, 2) * 16 + z * 4 + lax.div(y, 2) * 2 + c


def greet(devices):
    barrier = pltpu.get_barrier_semaphore()
    for device in devices:
        pl.semaphore_signal(barrier, inc=1, device_id=device, device_id_type=MESH)
    pl.semaphore_wait(barrier, len(devices))


def plane_neighbours(y, z, c):
    return [
        device_at(mod4(y + 1), z, c),
        device_at(mod4(y - 1), z, c),
        device_at(y, mod4(z + 1), c),
        device_at(y, mod4(z - 1), c),
        device_at(y, z, 1 - c),
    ]


STEPS = (0, -1, 1, 2)


def gather_kernel(items, n_in, *refs):
    ins, outs = refs[:n_in], refs[n_in : 2 * n_in]
    send_sems, recv_sems, local_sems = refs[2 * n_in :]
    y, z, c = where_am_i()
    up_y, dn_y, up_z, dn_z, partner = plane_neighbours(y, z, c)
    local = []
    for k in range(n_in):
        cp = pltpu.make_async_copy(ins[k], outs[k].at[block_at(y, z, c)], local_sems.at[k])
        cp.start()
        local.append(cp)
    greet([up_y, dn_y, up_z, dn_z, partner])
    started = []

    def item_ops(i):
        k, first, cols, y_first = items[i]
        up_u, dn_u, up_v, dn_v = (up_y, dn_y, up_z, dn_z) if y_first else (up_z, dn_z, up_y, dn_y)

        def block(du, dv):
            dy, dz = (du, dv) if y_first else (dv, du)
            return block_at(mod4(y + dy), mod4(z + dz), c)

        def part(half):
            if half is None:
                return pl.ds(first, cols)
            return pl.ds(first + half * (cols // 2), cols // 2)

        def send(ev, du, dv, half, device):
            place = outs[k].at[block(du, dv), :, part(half)]
            src = ins[k].at[:, part(half)] if (du, dv) == (0, 0) else place
            cp = pltpu.make_async_remote_copy(
                src_ref=src, dst_ref=place, send_sem=send_sems.at[i, ev], recv_sem=recv_sems.at[i, ev],
                device_id=device, device_id_type=MESH,
            )
            cp.start()
            started.append(cp)

        def arrive(ev, du, dv, half, core_flip=False):
            dy, dz = (du, dv) if y_first else (dv, du)
            b = block_at(mod4(y + dy), mod4(z + dz), 1 - c if core_flip else c)
            place = outs[k].at[b, :, part(half)]
            pltpu.make_async_remote_copy(
                src_ref=place, dst_ref=place, send_sem=send_sems.at[i, ev], recv_sem=recv_sems.at[i, ev],
                device_id=partner, device_id_type=MESH,
            ).wait_recv()

        def share(du, dv):
            send(20 + STEPS.index(du) * 4 + STEPS.index(dv), du, dv, None, partner)

        def shared(du, dv):
            arrive(20 + STEPS.index(du) * 4 + STEPS.index(dv), du, dv, None, True)

        def spread(du):
            base = 4 + 4 * STEPS.index(du)
            send(base, du, 0, None, up_v)
            send(base + 1, du, 0, None, dn_v)

        def relay(du):
            base = 4 + 4 * STEPS.index(du)
            arrive(base, du, -1, None)
            send(base + 2, du, -1, 0, up_v)
            share(du, -1)
            arrive(base + 1, du, 1, None)
            send(base + 3, du, 1, 1, dn_v)
            share(du, 1)

        def far(du):
            base = 4 + 4 * STEPS.index(du)
            arrive(base + 2, du, 2, 0)
            arrive(base + 3, du, 2, 1)
            share(du, 2)

        def s0():
            send(0, 0, 0, None, up_u)
            send(1, 0, 0, None, dn_u)
            spread(0)
            share(0, 0)

        def s1():
            arrive(0, -1, 0, None)
            send(2, -1, 0, 0, up_u)
            spread(-1)
            share(-1, 0)
            arrive(1, 1, 0, None)
            send(3, 1, 0, 1, dn_u)
            spread(1)
            share(1, 0)

        def s2():
            relay(0)

        def s3():
            arrive(2, 2, 0, 0)
            arrive(3, 2, 0, 1)
            spread(2)
            share(2, 0)

        def s4():
            relay(-1)
            relay(1)

        def s5():
            far(0)

        def s6():
            relay(2)

        def s7():
            far(-1)
            far(1)
            far(2)

        def s8():
            for du in STEPS:
                for dv in STEPS:
                    shared(du, dv)

        return [s0, s1, s2, s3, s4, s5, s6, s7, s8]

    stages = [item_ops(i) for i in range(len(items))]
    for s in range(9):
        for i in range(len(items)):
            stages[i][s]()
    for cp in started:
        cp.wait_send()
    for cp in local:
        cp.wait()


def plane_gather(arrays, items, collective_id):
    n = len(arrays)

    def body(*refs):
        gather_kernel(items, n, *refs)

    size = sum(a.size for a in arrays) * 2
    return pl.pallas_call(
        body,
        out_shape=[jax.ShapeDtypeStruct((32,) + a.shape, a.dtype) for a in arrays],
        in_specs=[pl.BlockSpec(memory_space=pltpu.VMEM)] * n,
        out_specs=[pl.BlockSpec(memory_space=pl.ANY)] * n,
        scratch_shapes=[
            pltpu.SemaphoreType.DMA((len(items), 36)),
            pltpu.SemaphoreType.DMA((len(items), 36)),
            pltpu.SemaphoreType.DMA((n,)),
        ],
        compiler_params=pltpu.CompilerParams(collective_id=collective_id, has_side_effects=True),
        cost_estimate=pl.CostEstimate(flops=0, bytes_accessed=64 * size, transcendentals=0),
        name="plane_gather",
    )(*arrays)


def scatter_kernel(n_items, *refs):
    ins, outs = refs[:n_items], refs[n_items : 2 * n_items]
    other, sums, near, total, last, send_sems, recv_sems = refs[2 * n_items :]
    y, z, c = where_am_i()
    up_y, dn_y, up_z, dn_z, partner = plane_neighbours(y, z, c)
    greet([up_y, dn_y, up_z, dn_z, partner])
    cols = ins[0].shape[2]
    halves = (pl.ds(0, cols // 2), pl.ds(cols // 2, cols // 2))
    started = []

    def copy(i, ev, src, dst, device):
        return pltpu.make_async_remote_copy(
            src_ref=src, dst_ref=dst, send_sem=send_sems.at[i, ev], recv_sem=recv_sems.at[i, ev],
            device_id=device, device_id_type=MESH,
        )

    def push(i, ev, src, dst, device):
        cp = copy(i, ev, src, dst, device)
        cp.start()
        started.append(cp)

    def added(a, b):
        return a.astype(jnp.float32) + b.astype(jnp.float32)

    def axes(i):
        return (up_y, dn_y, up_z, dn_z) if i % 2 == 0 else (up_z, dn_z, up_y, dn_y)

    def place(i, du, dv, core):
        dy, dz = (du, dv) if i % 2 == 0 else (dv, du)
        return block_at(mod4(y + dy), mod4(z + dz), core)

    order = [(du, dv) for dv in (2, 1, -1, 0) for du in (2, 1, -1, 0)]

    def slot(du, dv):
        return STEPS.index(du) * 4 + STEPS.index(dv)

    for du, dv in order:
        for i in range(n_items):
            s = slot(du, dv)
            push(i, s, ins[i].at[place(i, du, dv, 1 - c)], other.at[i, s], partner)

    def combine(i, du, dv):
        s = slot(du, dv)
        copy(i, s, other.at[i, s], other.at[i, s], partner).wait_recv()
        sums[i, s] = added(ins[i][place(i, du, dv, c)], other[i, s]).astype(jnp.bfloat16)

    def ring_far(i, base, box, src, up, dn):
        push(i, base, src.at[:, halves[0]], box.at[0, :, halves[0]], up)
        push(i, base + 1, src.at[:, halves[1]], box.at[0, :, halves[1]], dn)

    def ring_near(i, base, box, plus, minus, up, dn):
        spot = box.at[0, :, halves[0]]
        copy(i, base, spot, spot, up).wait_recv()
        plus[:, halves[0]] = added(plus[:, halves[0]], box[0, :, halves[0]]).astype(jnp.bfloat16)
        push(i, base + 2, plus, box.at[1], up)
        spot = box.at[0, :, halves[1]]
        copy(i, base + 1, spot, spot, dn).wait_recv()
        minus[:, halves[1]] = added(minus[:, halves[1]], box[0, :, halves[1]]).astype(jnp.bfloat16)
        push(i, base + 3, minus, box.at[2], dn)

    def ring_end(i, base, box, own):
        copy(i, base + 2, box.at[1], box.at[1], up_y).wait_recv()
        copy(i, base + 3, box.at[2], box.at[2], up_y).wait_recv()
        return added(own[...], box[1]) + box[2].astype(jnp.float32)

    back = (2, 1, -1, 0)
    for du in back:
        for i in range(n_items):
            _, _, up_v, dn_v = axes(i)
            combine(i, du, 2)
            k = STEPS.index(du)
            ring_far(i, 16 + 4 * k, near.at[i, k], sums.at[i, slot(du, 2)], up_v, dn_v)
    for du in back:
        for i in range(n_items):
            _, _, up_v, dn_v = axes(i)
            combine(i, du, 1)
            combine(i, du, -1)
            k = STEPS.index(du)
            ring_near(i, 16 + 4 * k, near.at[i, k], sums.at[i, slot(du, 1)], sums.at[i, slot(du, -1)], up_v, dn_v)
    for du in back:
        for i in range(n_items):
            up_u, dn_u, _, _ = axes(i)
            combine(i, du, 0)
            k = STEPS.index(du)
            got = ring_end(i, 16 + 4 * k, near.at[i, k], sums.at[i, slot(du, 0)])
            total[i, k] = got.astype(jnp.bfloat16)
            if du == 2:
                ring_far(i, 32, last.at[i], total.at[i, k], up_u, dn_u)
    for i in range(n_items):
        up_u, dn_u, _, _ = axes(i)
        ring_near(i, 32, last.at[i], total.at[i, STEPS.index(1)], total.at[i, STEPS.index(-1)], up_u, dn_u)
    for i in range(n_items):
        outs[i][...] = ring_end(i, 32, last.at[i], total.at[i, 0]).astype(outs[i].dtype)
    for cp in started:
        cp.wait_send()


def plane_scatter(arrays, dtypes, collective_id):
    n = len(arrays)
    rows, cols = arrays[0].shape[1:]

    def body(*refs):
        scatter_kernel(n, *refs)

    return pl.pallas_call(
        body,
        out_shape=[jax.ShapeDtypeStruct((rows, cols), d) for d in dtypes],
        in_specs=[pl.BlockSpec(memory_space=pltpu.VMEM)] * n,
        out_specs=[pl.BlockSpec(memory_space=pltpu.VMEM)] * n,
        scratch_shapes=[
            pltpu.VMEM((n, 16, rows, cols), jnp.bfloat16),
            pltpu.VMEM((n, 16, rows, cols), jnp.bfloat16),
            pltpu.VMEM((n, 4, 3, rows, cols), jnp.bfloat16),
            pltpu.VMEM((n, 4, rows, cols), jnp.bfloat16),
            pltpu.VMEM((n, 3, rows, cols), jnp.bfloat16),
            pltpu.SemaphoreType.DMA((n, 36)),
            pltpu.SemaphoreType.DMA((n, 36)),
        ],
        compiler_params=pltpu.CompilerParams(
            collective_id=collective_id, has_side_effects=True, vmem_limit_bytes=VMEM_CAP
        ),
        name="plane_scatter",
    )(*arrays)


TILE = 128


def output_kernel(
    loss_scale, width,
    mixed, outw, student, target, gain,
    layer, pre, mixed_all, mixed_grad,
    summed, parts, boxes, stat_out, stat_in,
    send_sems, recv_sems,
):
    me = lax.axis_index("tensor")
    rows = mixed.shape[0]
    tiles = rows // TILE
    up, dn, opp = ({"tensor": mod4(me + d)} for d in (1, -1, 2))
    t_dn, t_up, t_far = mod4(me - 1), mod4(me + 1), mod4(me + 2)
    greet([up, dn, opp])
    started = []

    def copy(ev, src, dst, device):
        return pltpu.make_async_remote_copy(
            src_ref=src, dst_ref=dst, send_sem=send_sems.at[ev], recv_sem=recv_sems.at[ev],
            device_id=device, device_id_type=MESH,
        )

    def push(ev, src, dst, device):
        cp = copy(ev, src, dst, device)
        cp.start()
        started.append(cp)

    half = rows // 2
    halves = (pl.ds(0, half), pl.ds(half, half))
    push(0, mixed, mixed_all.at[me], up)
    push(1, mixed, mixed_all.at[me], dn)

    def project(t, first, source):
        @pl.loop(0, tiles)
        def _(i):
            at = pl.ds(pl.multiple_of(i * TILE, TILE), TILE)
            got = lax.dot_general(
                source[at, :], outw[t], (((1,), (1,)), ((), ())), preferred_element_type=jnp.float32
            )
            if first:
                summed[at, :] = got
            else:
                summed[at, :] += got

    project(me, True, mixed)
    mixed_all[me] = mixed[...]
    copy(0, mixed, mixed_all.at[t_dn], up).wait_recv()
    push(2, mixed_all.at[t_dn, halves[0]], mixed_all.at[t_dn, halves[0]], up)
    copy(1, mixed, mixed_all.at[t_up], dn).wait_recv()
    push(3, mixed_all.at[t_up, halves[1]], mixed_all.at[t_up, halves[1]], dn)
    project(t_dn, False, mixed_all.at[t_dn])
    project(t_up, False, mixed_all.at[t_up])
    for h in (0, 1):
        spot = mixed_all.at[t_far, halves[h]]
        copy(2 + h, spot, spot, up).wait_recv()
    project(t_far, False, mixed_all.at[t_far])

    def exchange(ev, k, fill):
        @pl.loop(0, tiles)
        def _(i):
            at = pl.ds(pl.multiple_of(i * TILE, TILE), TILE)
            column = fill(at)
            stat_out[k, :, at] = jnp.transpose(jnp.broadcast_to(column, (TILE, TILE)))[:8]

        for j, device in enumerate((up, dn, opp)):
            push(ev + j, stat_out.at[k], stat_in.at[k, j], device)
        for j, device in enumerate((up, dn, opp)):
            copy(ev + j, stat_out.at[k], stat_in.at[k, j], device).wait_recv()

    def whole_mean(k, at):
        row = stat_out[k, :, at] + stat_in[k, 0, :, at] + stat_in[k, 1, :, at] + stat_in[k, 2, :, at]
        column = jnp.transpose(jnp.broadcast_to(row[:1], (TILE, TILE)))[:, :1]
        return column * (1.0 / width)

    def squares(at):
        s = summed[at, :]
        return jnp.sum(s * s, axis=1, keepdims=True)

    exchange(4, 0, squares)

    def scaled_grad(at):
        return gain[...] * (loss_scale * (layer[at, :].astype(jnp.float32) - target[at, :].astype(jnp.float32)))

    def crossed(at):
        factor = lax.rsqrt(whole_mean(0, at) + norm_eps)
        s = summed[at, :]
        layer[at, :] = (student[at, :].astype(jnp.float32) + s * factor * gain[...]).astype(jnp.bfloat16)
        return jnp.sum(s * scaled_grad(at), axis=1, keepdims=True)

    exchange(7, 1, crossed)

    @pl.loop(0, tiles)
    def _(i):
        at = pl.ds(pl.multiple_of(i * TILE, TILE), TILE)
        factor = lax.rsqrt(whole_mean(0, at) + norm_eps)
        along = whole_mean(1, at)
        pre[at, :] = (
            factor * scaled_grad(at) - summed[at, :] * (factor * factor * factor * along)
        ).astype(jnp.bfloat16)

    def pull(t, k):
        @pl.loop(0, tiles)
        def _(i):
            at = pl.ds(pl.multiple_of(i * TILE, TILE), TILE)
            parts[k, at, :] = jnp.dot(
                pre[at, :], outw[t], preferred_element_type=jnp.float32
            ).astype(jnp.bfloat16)

    def added(a, b):
        return a.astype(jnp.float32) + b.astype(jnp.float32)

    pull(t_far, 2)
    push(10, parts.at[2, halves[0]], boxes.at[0, halves[0]], up)
    push(11, parts.at[2, halves[1]], boxes.at[0, halves[1]], dn)
    pull(t_up, 1)
    pull(t_dn, 3)
    spot = boxes.at[0, halves[0]]
    copy(10, spot, spot, up).wait_recv()
    parts[1, halves[0], :] = added(parts[1, halves[0], :], boxes[0, halves[0], :]).astype(jnp.bfloat16)
    push(12, parts.at[1], boxes.at[1], up)
    spot = boxes.at[0, halves[1]]
    copy(11, spot, spot, dn).wait_recv()
    parts[3, halves[1], :] = added(parts[3, halves[1], :], boxes[0, halves[1], :]).astype(jnp.bfloat16)
    push(13, parts.at[3], boxes.at[2], dn)
    pull(me, 0)
    copy(12, boxes.at[1], boxes.at[1], up).wait_recv()
    copy(13, boxes.at[2], boxes.at[2], dn).wait_recv()
    mixed_grad[...] = (added(parts[0], boxes[1]) + boxes[2].astype(jnp.float32)).astype(jnp.bfloat16)
    for cp in started:
        cp.wait_send()


def output_stage(mixed, outw, student, target, gain, loss_scale, width, collective_id):
    rows, cols = mixed.shape
    share = student.shape[1]

    def body(*refs):
        output_kernel(loss_scale, width, *refs)

    bf16 = jnp.bfloat16
    return pl.pallas_call(
        body,
        out_shape=[
            jax.ShapeDtypeStruct((rows, share), bf16),
            jax.ShapeDtypeStruct((rows, share), bf16),
            jax.ShapeDtypeStruct((4, rows, cols), bf16),
            jax.ShapeDtypeStruct((rows, cols), bf16),
        ],
        in_specs=[pl.BlockSpec(memory_space=pltpu.VMEM)] * 5,
        out_specs=[pl.BlockSpec(memory_space=pltpu.VMEM)] * 4,
        scratch_shapes=[
            pltpu.VMEM((rows, share), jnp.float32),
            pltpu.VMEM((4, rows, cols), bf16),
            pltpu.VMEM((3, rows, cols), bf16),
            pltpu.VMEM((2, 8, rows), jnp.float32),
            pltpu.VMEM((2, 3, 8, rows), jnp.float32),
            pltpu.SemaphoreType.DMA((14,)),
            pltpu.SemaphoreType.DMA((14,)),
        ],
        compiler_params=pltpu.CompilerParams(
            collective_id=collective_id, has_side_effects=True, vmem_limit_bytes=VMEM_CAP
        ),
        name="output_stage",
    )(mixed, outw, student, target, gain)


def from_partner(block, axis, bit):
    count = lax.axis_size(axis)
    route = []
    for low in range(count):
        high = low | 1 << bit
        if high != low and high < count:
            route += [(low, high), (high, low)]
    return lax.ppermute(block, axis, route)


def from_behind(x, axis, by):
    count = lax.axis_size(axis)
    pairs = [(i, i + by) for i in range(count) if 0 <= i + by < count]
    return lax.ppermute(x, axis, pairs)


def swap_share(block):
    route = []
    for sec in range(2):
        for dp in range(16):
            for t in range(4):
                high, low = dp // 8, dp % 8
                there = ((t // 2) * 16 + (t % 2) * 8 + low) * 4 + sec * 2 + high
                route.append(((sec * 16 + dp) * 4 + t, there))
    return lax.ppermute(block, ("sec", "dp", "tensor"), route)


def rotate(values, cos_table, sin_table, sign_value):
    row_count = values.shape[0]
    half_dim = cos_table.shape[1]
    per_head = values.reshape(row_count, -1, 2 * half_dim)
    leading = per_head[:, :, :half_dim]
    trailing = per_head[:, :, half_dim:]
    cosines = cos_table[:, None, :]
    sin_scaled = sign_value * sin_table[:, None, :]
    rotated = jnp.concatenate(
        [leading * cosines - trailing * sin_scaled, trailing * cosines + leading * sin_scaled],
        axis=2,
    )
    return rotated.reshape(row_count, -1)


def shards(
    student_rows,
    teacher_rows,
    norm_gain,
    post_gain,
    query_weight,
    key_weight,
    value_weight,
    out_weight,
):
    f32, bf16 = jnp.float32, jnp.bfloat16
    tok_count = student_rows.shape[1]
    model_width = student_rows.shape[2]
    tensor_count = lax.axis_size("tensor")
    share_cols = model_width // tensor_count
    data_count = lax.axis_size("sec") * lax.axis_size("dp")
    blocks_back = (W + tok_count - 1) // tok_count
    key_count = (blocks_back + 1) * tok_count
    local_groups = key_weight.shape[1] // HD
    group_size = HEADS // KV_HEADS
    query_cols = query_weight.shape[1]
    kv_cols = key_weight.shape[1]
    score_scale = 1.0 / math.sqrt(HD)
    loss_scale = 2.0 / math.sqrt(data_count * tok_count)
    share_start = lax.axis_index("tensor") * share_cols

    def share_of(x, axis):
        return lax.dynamic_slice_in_dim(x, share_start, share_cols, axis)

    out_block = swap_share(out_weight)
    key_value = jnp.concatenate([key_weight, value_weight], axis=1)
    items = ((0, 0, 512, True), (1, 0, 512, False), (2, 0, 256, True), (2, 256, 256, False))
    query_full, kv_full, out_share = plane_gather((query_weight, key_value, out_block), items, 0)
    query_full = query_full.reshape(model_width, query_cols)
    kv_full = kv_full.reshape(model_width, 2 * kv_cols)
    out_share = out_share.reshape(tensor_count, share_cols, query_cols)
    teacher_share, kv_full = lax.optimization_barrier((share_of(teacher_rows[0], 1), kv_full))
    target = from_partner(teacher_share, "sec", 0)

    student_f = student_rows[0].astype(f32)
    inverse = lax.rsqrt(jnp.mean(student_f * student_f, axis=1, keepdims=True) + norm_eps)
    normed = (student_f * inverse * norm_gain).astype(bf16)
    first_pos = lax.axis_index("dp") * tok_count
    half_dim = HD // 2
    inv_freq = jnp.power(f32(rope_base), -2.0 * jnp.arange(half_dim, dtype=f32) / HD)
    positions = (first_pos + jnp.arange(tok_count, dtype=jnp.int32)).astype(f32)
    angles = positions[:, None] * inv_freq[None, :]
    cos_table = jnp.cos(angles)
    sin_table = jnp.sin(angles)
    key_values = jnp.dot(normed, kv_full, preferred_element_type=f32)
    key_rows = rotate(key_values[:, :kv_cols], cos_table, sin_table, 1.0).astype(bf16)
    value_rows = key_values[:, kv_cols:].astype(bf16)
    key_parts = [key_rows]
    value_parts = [value_rows]
    for offset in range(1, blocks_back + 1):
        earlier_keys, earlier_values = from_behind((key_rows, value_rows), "dp", offset)
        key_parts = [earlier_keys] + key_parts
        value_parts = [earlier_values] + value_parts
    queries = rotate(
        jnp.dot(normed, query_full, preferred_element_type=f32), cos_table, sin_table, 1.0
    ).astype(bf16)
    key_window = jnp.concatenate(key_parts, axis=0)
    value_window = jnp.concatenate(value_parts, axis=0)
    query_pos = first_pos + jnp.arange(tok_count, dtype=jnp.int32)
    key_pos = first_pos - blocks_back * tok_count + jnp.arange(key_count, dtype=jnp.int32)
    allowed = (
        (key_pos[None, :] >= 0)
        & (key_pos[None, :] <= query_pos[:, None])
        & (key_pos[None, :] > query_pos[:, None] - W)
    )
    grouped_q = queries.reshape(tok_count, local_groups, group_size, HD)
    grouped_k = key_window.reshape(key_count, local_groups, HD)
    grouped_v = value_window.reshape(key_count, local_groups, HD)
    scores = jnp.einsum("tgad,kgd->gatk", grouped_q, grouped_k, preferred_element_type=f32) * score_scale
    scores = jnp.where(allowed, scores, masked_score)
    row_peak = jnp.max(scores, axis=3, keepdims=True)
    exp_scores = jnp.exp(scores - row_peak)
    attn_probs = exp_scores / jnp.sum(exp_scores, axis=3, keepdims=True)
    probs_b = attn_probs.astype(bf16)
    mixed_rows = (
        jnp.einsum("gatk,kgd->tgad", probs_b, grouped_v, preferred_element_type=f32)
        .astype(bf16)
        .reshape(tok_count, query_cols)
    )
    layer_share, pre_share, mixed_all, mixed_grad = output_stage(
        mixed_rows, out_share, share_of(student_rows[0], 1), target, share_of(post_gain, 0)[None],
        loss_scale, float(model_width), 1,
    )
    grouped_g = mixed_grad.reshape(tok_count, local_groups, group_size, HD)
    prob_grad = jnp.einsum("tgad,kgd->gatk", grouped_g, grouped_v, preferred_element_type=f32)
    score_grad = (
        attn_probs * (prob_grad - jnp.sum(attn_probs * prob_grad, axis=3, keepdims=True))
    ).astype(bf16)
    rotated_grad = (
        jnp.einsum("gatk,kgd->tgad", score_grad, grouped_k, preferred_element_type=f32).reshape(
            tok_count, query_cols
        )
        * score_scale
    )
    query_pre = rotate(rotated_grad, cos_table, sin_table, -1.0).astype(bf16)
    query_term = jnp.einsum("td,te->de", normed, query_pre, preferred_element_type=f32).astype(bf16)
    out_term = jnp.einsum("td,ate->ade", pre_share, mixed_all, preferred_element_type=f32).astype(bf16)
    query_grad, out_grad = plane_scatter(
        (query_term.reshape(32, -1, query_cols), out_term.reshape(32, -1, query_cols)), (f32, bf16), 2
    )
    return (layer_share[None], query_grad, swap_share(out_grad).astype(f32))


def solution(mesh):
    in_specs = (
        P("sec", "dp", None),
        P("sec", "dp", None),
        P(),
        P(),
        P(("sec", "dp"), "tensor"),
        P(("sec", "dp"), "tensor"),
        P(("sec", "dp"), "tensor"),
        P(("sec", "dp"), "tensor"),
    )
    out_specs = (P("sec", "dp", "tensor"), P(("sec", "dp"), "tensor"), P(("sec", "dp"), "tensor"))
    return jax.shard_map(shards, mesh=mesh, in_specs=in_specs, out_specs=out_specs, check_vma=False)
```

```python
import math

import jax
import jax.numpy as jnp
from jax import lax
from jax.experimental import pallas as pl
from jax.experimental.pallas import tpu as pltpu
from jax.sharding import PartitionSpec as P

HD = 256
W = 1024
MESH = pl.DeviceIdType.MESH
VMEM_CAP = 60 * 1024 * 1024

norm_eps = 1e-06
rope_base = 10000.0
masked_score = -1e30


def where_am_i():
    sec, dp = lax.axis_index("sec"), lax.axis_index("dp")
    z = lax.div(dp, 4)
    y = lax.rem(lax.div(dp, 2), 2) * 2 + sec
    return y, z, lax.rem(dp, 2)


def mod4(v):
    return lax.rem(v + 4, 4)


def device_at(y, z, c):
    return {"sec": lax.rem(y, 2), "dp": z * 4 + lax.div(y, 2) * 2 + c}


def block_at(y, z, c):
    return lax.rem(y, 2) * 16 + z * 4 + lax.div(y, 2) * 2 + c


def greet(devices):
    barrier = pltpu.get_barrier_semaphore()
    for device in devices:
        pl.semaphore_signal(barrier, inc=1, device_id=device, device_id_type=MESH)
    pl.semaphore_wait(barrier, len(devices))


def plane_neighbours(y, z, c):
    return [
        device_at(mod4(y + 1), z, c),
        device_at(mod4(y - 1), z, c),
        device_at(y, mod4(z + 1), c),
        device_at(y, mod4(z - 1), c),
        device_at(y, z, 1 - c),
    ]


STEPS = (0, -1, 1, 2)


def gather_kernel(items, n_in, *refs):
    ins, outs = refs[:n_in], refs[n_in : 2 * n_in]
    send_sems, recv_sems, local_sems = refs[2 * n_in :]
    y, z, c = where_am_i()
    up_y, dn_y, up_z, dn_z, partner = plane_neighbours(y, z, c)
    local = []
    for k in range(n_in):
        cp = pltpu.make_async_copy(ins[k], outs[k].at[block_at(y, z, c)], local_sems.at[k])
        cp.start()
        local.append(cp)
    greet([up_y, dn_y, up_z, dn_z, partner])
    started = []

    def item_ops(i):
        k, first, cols, y_first = items[i]
        up_u, dn_u, up_v, dn_v = (up_y, dn_y, up_z, dn_z) if y_first else (up_z, dn_z, up_y, dn_y)

        def block(du, dv):
            dy, dz = (du, dv) if y_first else (dv, du)
            return block_at(mod4(y + dy), mod4(z + dz), c)

        def part(half):
            if half is None:
                return pl.ds(first, cols)
            return pl.ds(first + half * (cols // 2), cols // 2)

        def send(ev, du, dv, half, device):
            place = outs[k].at[block(du, dv), :, part(half)]
            src = ins[k].at[:, part(half)] if (du, dv) == (0, 0) else place
            cp = pltpu.make_async_remote_copy(
                src_ref=src, dst_ref=place, send_sem=send_sems.at[i, ev], recv_sem=recv_sems.at[i, ev],
                device_id=device, device_id_type=MESH,
            )
            cp.start()
            started.append(cp)

        def arrive(ev, du, dv, half, core_flip=False):
            dy, dz = (du, dv) if y_first else (dv, du)
            b = block_at(mod4(y + dy), mod4(z + dz), 1 - c if core_flip else c)
            place = outs[k].at[b, :, part(half)]
            pltpu.make_async_remote_copy(
                src_ref=place, dst_ref=place, send_sem=send_sems.at[i, ev], recv_sem=recv_sems.at[i, ev],
                device_id=partner, device_id_type=MESH,
            ).wait_recv()

        def share(du, dv):
            send(20 + STEPS.index(du) * 4 + STEPS.index(dv), du, dv, None, partner)

        def shared(du, dv):
            arrive(20 + STEPS.index(du) * 4 + STEPS.index(dv), du, dv, None, True)

        def spread(du):
            base = 4 + 4 * STEPS.index(du)
            send(base, du, 0, None, up_v)
            send(base + 1, du, 0, None, dn_v)

        def relay(du):
            base = 4 + 4 * STEPS.index(du)
            arrive(base, du, -1, None)
            send(base + 2, du, -1, 0, up_v)
            share(du, -1)
            arrive(base + 1, du, 1, None)
            send(base + 3, du, 1, 1, dn_v)
            share(du, 1)

        def far(du):
            base = 4 + 4 * STEPS.index(du)
            arrive(base + 2, du, 2, 0)
            arrive(base + 3, du, 2, 1)
            share(du, 2)

        def s0():
            send(0, 0, 0, None, up_u)
            send(1, 0, 0, None, dn_u)
            spread(0)
            share(0, 0)

        def s1():
            arrive(0, -1, 0, None)
            send(2, -1, 0, 0, up_u)
            spread(-1)
            share(-1, 0)
            arrive(1, 1, 0, None)
            send(3, 1, 0, 1, dn_u)
            spread(1)
            share(1, 0)

        def s2():
            relay(0)

        def s3():
            arrive(2, 2, 0, 0)
            arrive(3, 2, 0, 1)
            spread(2)
            share(2, 0)

        def s4():
            relay(-1)
            relay(1)

        def s5():
            far(0)

        def s6():
            relay(2)

        def s7():
            far(-1)
            far(1)
            far(2)

        def s8():
            for du in STEPS:
                for dv in STEPS:
                    shared(du, dv)

        return [s0, s1, s2, s3, s4, s5, s6, s7, s8]

    stages = [item_ops(i) for i in range(len(items))]
    for s in range(9):
        for i in range(len(items)):
            stages[i][s]()
    for cp in started:
        cp.wait_send()
    for cp in local:
        cp.wait()


def plane_gather(arrays, items, collective_id):
    n = len(arrays)

    def body(*refs):
        gather_kernel(items, n, *refs)

    size = sum(a.size for a in arrays) * 2
    return pl.pallas_call(
        body,
        out_shape=[jax.ShapeDtypeStruct((32,) + a.shape, a.dtype) for a in arrays],
        in_specs=[pl.BlockSpec(memory_space=pltpu.VMEM)] * n,
        out_specs=[pl.BlockSpec(memory_space=pl.ANY)] * n,
        scratch_shapes=[
            pltpu.SemaphoreType.DMA((len(items), 36)),
            pltpu.SemaphoreType.DMA((len(items), 36)),
            pltpu.SemaphoreType.DMA((n,)),
        ],
        compiler_params=pltpu.CompilerParams(collective_id=collective_id, has_side_effects=True),
        cost_estimate=pl.CostEstimate(flops=0, bytes_accessed=64 * size, transcendentals=0),
        name="plane_gather",
    )(*arrays)


def scatter_kernel(n_items, *refs):
    ins, outs = refs[:n_items], refs[n_items : 2 * n_items]
    other, sums, near, total, last, send_sems, recv_sems = refs[2 * n_items :]
    y, z, c = where_am_i()
    up_y, dn_y, up_z, dn_z, partner = plane_neighbours(y, z, c)
    greet([up_y, dn_y, up_z, dn_z, partner])
    cols = ins[0].shape[2]
    halves = (pl.ds(0, cols // 2), pl.ds(cols // 2, cols // 2))
    started = []

    def copy(i, ev, src, dst, device):
        return pltpu.make_async_remote_copy(
            src_ref=src, dst_ref=dst, send_sem=send_sems.at[i, ev], recv_sem=recv_sems.at[i, ev],
            device_id=device, device_id_type=MESH,
        )

    def push(i, ev, src, dst, device):
        cp = copy(i, ev, src, dst, device)
        cp.start()
        started.append(cp)

    def added(a, b):
        return a.astype(jnp.float32) + b.astype(jnp.float32)

    def axes(i):
        return (up_y, dn_y, up_z, dn_z) if i % 2 == 0 else (up_z, dn_z, up_y, dn_y)

    def place(i, du, dv, core):
        dy, dz = (du, dv) if i % 2 == 0 else (dv, du)
        return block_at(mod4(y + dy), mod4(z + dz), core)

    order = [(du, dv) for dv in (2, 1, -1, 0) for du in (2, 1, -1, 0)]

    def slot(du, dv):
        return STEPS.index(du) * 4 + STEPS.index(dv)

    for du, dv in order:
        for i in range(n_items):
            s = slot(du, dv)
            push(i, s, ins[i].at[place(i, du, dv, 1 - c)], other.at[i, s], partner)

    def combine(i, du, dv):
        s = slot(du, dv)
        copy(i, s, other.at[i, s], other.at[i, s], partner).wait_recv()
        sums[i, s] = added(ins[i][place(i, du, dv, c)], other[i, s]).astype(jnp.bfloat16)

    def ring_far(i, base, box, src, up, dn):
        push(i, base, src.at[:, halves[0]], box.at[0, :, halves[0]], up)
        push(i, base + 1, src.at[:, halves[1]], box.at[0, :, halves[1]], dn)

    def ring_near(i, base, box, plus, minus, up, dn):
        spot = box.at[0, :, halves[0]]
        copy(i, base, spot, spot, up).wait_recv()
        plus[:, halves[0]] = added(plus[:, halves[0]], box[0, :, halves[0]]).astype(jnp.bfloat16)
        push(i, base + 2, plus, box.at[1], up)
        spot = box.at[0, :, halves[1]]
        copy(i, base + 1, spot, spot, dn).wait_recv()
        minus[:, halves[1]] = added(minus[:, halves[1]], box[0, :, halves[1]]).astype(jnp.bfloat16)
        push(i, base + 3, minus, box.at[2], dn)

    def ring_end(i, base, box, own):
        copy(i, base + 2, box.at[1], box.at[1], up_y).wait_recv()
        copy(i, base + 3, box.at[2], box.at[2], up_y).wait_recv()
        return added(own[...], box[1]) + box[2].astype(jnp.float32)

    back = (2, 1, -1, 0)
    for du in back:
        for i in range(n_items):
            _, _, up_v, dn_v = axes(i)
            combine(i, du, 2)
            k = STEPS.index(du)
            ring_far(i, 16 + 4 * k, near.at[i, k], sums.at[i, slot(du, 2)], up_v, dn_v)
    for du in back:
        for i in range(n_items):
            _, _, up_v, dn_v = axes(i)
            combine(i, du, 1)
            combine(i, du, -1)
            k = STEPS.index(du)
            ring_near(i, 16 + 4 * k, near.at[i, k], sums.at[i, slot(du, 1)], sums.at[i, slot(du, -1)], up_v, dn_v)
    for du in back:
        for i in range(n_items):
            up_u, dn_u, _, _ = axes(i)
            combine(i, du, 0)
            k = STEPS.index(du)
            got = ring_end(i, 16 + 4 * k, near.at[i, k], sums.at[i, slot(du, 0)])
            total[i, k] = got.astype(jnp.bfloat16)
            if du == 2:
                ring_far(i, 32, last.at[i], total.at[i, k], up_u, dn_u)
    for i in range(n_items):
        up_u, dn_u, _, _ = axes(i)
        ring_near(i, 32, last.at[i], total.at[i, STEPS.index(1)], total.at[i, STEPS.index(-1)], up_u, dn_u)
    for i in range(n_items):
        outs[i][...] = ring_end(i, 32, last.at[i], total.at[i, 0]).astype(outs[i].dtype)
    for cp in started:
        cp.wait_send()


def plane_scatter(arrays, dtypes, collective_id):
    n = len(arrays)
    rows, cols = arrays[0].shape[1:]

    def body(*refs):
        scatter_kernel(n, *refs)

    return pl.pallas_call(
        body,
        out_shape=[jax.ShapeDtypeStruct((rows, cols), d) for d in dtypes],
        in_specs=[pl.BlockSpec(memory_space=pltpu.VMEM)] * n,
        out_specs=[pl.BlockSpec(memory_space=pltpu.VMEM)] * n,
        scratch_shapes=[
            pltpu.VMEM((n, 16, rows, cols), jnp.bfloat16),
            pltpu.VMEM((n, 16, rows, cols), jnp.bfloat16),
            pltpu.VMEM((n, 4, 3, rows, cols), jnp.bfloat16),
            pltpu.VMEM((n, 4, rows, cols), jnp.bfloat16),
            pltpu.VMEM((n, 3, rows, cols), jnp.bfloat16),
            pltpu.SemaphoreType.DMA((n, 36)),
            pltpu.SemaphoreType.DMA((n, 36)),
        ],
        compiler_params=pltpu.CompilerParams(
            collective_id=collective_id, has_side_effects=True, vmem_limit_bytes=VMEM_CAP
        ),
        name="plane_scatter",
    )(*arrays)


TILE = 128


def core_kernel(
    loss_scale, score_scale, width,
    queries, keys, values, outw, student, teacher, gain, cosines, sines,
    layer, pre, mixed_all, query_pre,
    summed, probs, parts, boxes, stud, targ, stat_out, stat_in,
    send_sems, recv_sems, side_sems,
):
    f32, bf16 = jnp.float32, jnp.bfloat16
    me, sec, dp = lax.axis_index("tensor"), lax.axis_index("sec"), lax.axis_index("dp")
    rows, head = queries.shape[0], keys.shape[1]
    share = layer.shape[1]
    wide = stud.shape[1]
    window = W + TILE
    tiles = rows // TILE
    half_tile = TILE // 2
    up, dn, opp = ({"tensor": mod4(me + d)} for d in (1, -1, 2))
    t_dn, t_up, t_far = mod4(me - 1), mod4(me + 1), mod4(me + 2)
    odd = lax.rem(me, 2)
    begin = pl.multiple_of(lax.div(me, 2) * (2 * share) + odd * (2 * share - wide), 128)
    pair = {"sec": 1 - sec}

    mine = pltpu.make_async_copy(student.at[:, pl.ds(begin, wide)], stud, side_sems.at[0])
    mine.start()
    greet([up, dn, opp, pair])
    theirs = pltpu.make_async_remote_copy(
        src_ref=teacher.at[:, pl.ds(begin, wide)], dst_ref=targ, send_sem=side_sems.at[1],
        recv_sem=side_sems.at[2], device_id=pair, device_id_type=MESH,
    )
    theirs.start()
    started = []

    def copy(i, ev, src, dst, device):
        return pltpu.make_async_remote_copy(
            src_ref=src, dst_ref=dst, send_sem=send_sems.at[i, ev], recv_sem=recv_sems.at[i, ev],
            device_id=device, device_id_type=MESH,
        )

    def push(i, ev, src, dst, device):
        cp = copy(i, ev, src, dst, device)
        cp.start()
        started.append(cp)

    def arrive(i, ev, spot):
        copy(i, ev, spot, spot, up).wait_recv()

    def lanes(x):
        return jnp.where(odd == 1, x[:, wide - share :], x[:, :share])

    def gains():
        return lanes(gain[:, pl.ds(begin, wide)])

    def nt(a, b):
        return lax.dot_general(a, b, (((1,), (1,)), ((), ())), preferred_element_type=f32)

    def added(a, b):
        return a.astype(f32) + b.astype(f32)

    def both(ref, at):
        return jnp.concatenate([ref[at, :head], ref[at, head:]], axis=0)

    def at_of(i):
        return pl.ds(i * TILE, TILE)

    def halves_of(i):
        return pl.ds(i * TILE, half_tile), pl.ds(i * TILE + half_tile, half_tile)

    def attend(i):
        at = at_of(i)
        near = pl.ds(i * TILE, window)
        scores = nt(both(queries, at), keys[near, :]) * score_scale
        row = lax.rem(lax.broadcasted_iota(jnp.int32, scores.shape, 0), TILE)
        col = lax.broadcasted_iota(jnp.int32, scores.shape, 1)
        allowed = (col > row) & (col - W <= row) & (col >= W - i * TILE - rows * dp)
        scores = jnp.where(allowed, scores, masked_score)
        weights = jnp.exp(scores - jnp.max(scores, axis=1, keepdims=True))
        prob = weights * (1.0 / jnp.sum(weights, axis=1, keepdims=True))
        probs[i] = prob
        mix = jnp.dot(prob.astype(bf16), values[near, :], preferred_element_type=f32).astype(bf16)
        mixed_all[me, at, :head] = mix[:TILE]
        mixed_all[me, at, head:] = mix[TILE:]
        push(i, 0, mixed_all.at[me, at], mixed_all.at[me, at], up)
        push(i, 1, mixed_all.at[me, at], mixed_all.at[me, at], dn)

    def relay(i):
        at = at_of(i)
        h0, h1 = halves_of(i)
        arrive(i, 0, mixed_all.at[t_dn, at])
        push(i, 2, mixed_all.at[t_dn, h0], mixed_all.at[t_dn, h0], up)
        arrive(i, 1, mixed_all.at[t_up, at])
        push(i, 3, mixed_all.at[t_up, h1], mixed_all.at[t_up, h1], dn)

    def send_stat(i, k, column):
        at = at_of(i)
        stat_out[k, :, at] = jnp.transpose(jnp.broadcast_to(column, (TILE, 128)))[:8]
        for j, device in enumerate((up, dn, opp)):
            push(i, 4 + 3 * k + j, stat_out.at[k, :, at], stat_in.at[k, j, :, at], device)

    def wait_stat(i, k):
        for j in range(3):
            arrive(i, 4 + 3 * k + j, stat_in.at[k, j, :, at_of(i)])

    def whole_mean(i, k):
        at = at_of(i)
        row = stat_out[k, :, at] + stat_in[k, 0, :, at] + stat_in[k, 1, :, at] + stat_in[k, 2, :, at]
        column = jnp.transpose(jnp.broadcast_to(row[:1], (128, TILE)))[:, :1]
        return column * (1.0 / width)

    def project(i):
        at = at_of(i)
        h0, h1 = halves_of(i)
        got = nt(mixed_all[me, at, :], outw[me])
        got += nt(mixed_all[t_dn, at, :], outw[t_dn])
        got += nt(mixed_all[t_up, at, :], outw[t_up])
        arrive(i, 2, mixed_all.at[t_far, h0])
        arrive(i, 3, mixed_all.at[t_far, h1])
        got += nt(mixed_all[t_far, at, :], outw[t_far])
        summed[at, :] = got
        send_stat(i, 0, jnp.sum(got * got, axis=1, keepdims=True))

    def scaled_grad(at):
        return gains() * (loss_scale * (layer[at, :].astype(f32) - lanes(targ[at, :].astype(f32))))

    def finish(i):
        at = at_of(i)
        if i == 0:
            mine.wait()
        wait_stat(i, 0)
        factor = lax.rsqrt(whole_mean(i, 0) + norm_eps)
        s = summed[at, :]
        layer[at, :] = (lanes(stud[at, :].astype(f32)) + s * factor * gains()).astype(bf16)
        if i == 0:
            theirs.wait_recv()
        send_stat(i, 1, jnp.sum(s * scaled_grad(at), axis=1, keepdims=True))

    def pull(i, t, k):
        at = at_of(i)
        parts[k, at, :] = jnp.dot(pre[at, :], outw[t], preferred_element_type=f32).astype(bf16)

    def back(i):
        at = at_of(i)
        h0, h1 = halves_of(i)
        wait_stat(i, 1)
        factor = lax.rsqrt(whole_mean(i, 0) + norm_eps)
        along = whole_mean(i, 1)
        pre[at, :] = (
            factor * scaled_grad(at) - summed[at, :] * (factor * factor * factor * along)
        ).astype(bf16)
        pull(i, t_far, 2)
        push(i, 10, parts.at[2, h0], boxes.at[0, h0], up)
        push(i, 11, parts.at[2, h1], boxes.at[0, h1], dn)
        pull(i, t_up, 1)
        pull(i, t_dn, 3)

    def merge(i):
        at = at_of(i)
        h0, h1 = halves_of(i)
        arrive(i, 10, boxes.at[0, h0])
        parts[1, h0, :] = added(parts[1, h0, :], boxes[0, h0, :]).astype(bf16)
        push(i, 12, parts.at[1, at], boxes.at[1, at], up)
        arrive(i, 11, boxes.at[0, h1])
        parts[3, h1, :] = added(parts[3, h1, :], boxes[0, h1, :]).astype(bf16)
        push(i, 13, parts.at[3, at], boxes.at[2, at], dn)

    def attend_back(i):
        at = at_of(i)
        near = pl.ds(i * TILE, window)
        own = jnp.dot(pre[at, :], outw[me], preferred_element_type=f32)
        arrive(i, 12, boxes.at[1, at])
        arrive(i, 13, boxes.at[2, at])
        grad = (own + added(boxes[1, at, :], boxes[2, at, :])).astype(bf16)
        grad = jnp.concatenate([grad[:, :head], grad[:, head:]], axis=0)
        prob_grad = nt(grad, values[near, :])
        prob = probs[i]
        score_grad = (prob * (prob_grad - jnp.sum(prob * prob_grad, axis=1, keepdims=True))).astype(bf16)
        rotated = jnp.dot(score_grad, keys[near, :], preferred_element_type=f32) * score_scale
        cos, sin = cosines[at, :], sines[at, :]
        half = head // 2
        for h in range(2):
            lead = rotated[h * TILE : (h + 1) * TILE, :half]
            trail = rotated[h * TILE : (h + 1) * TILE, half:]
            query_pre[at, h * head : h * head + half] = (lead * cos + trail * sin).astype(bf16)
            query_pre[at, h * head + half : (h + 1) * head] = (trail * cos - lead * sin).astype(bf16)

    stages = (attend, relay, project, finish, back, merge, attend_back)
    for step in range(tiles + len(stages) - 1):
        for k, stage in enumerate(stages):
            if 0 <= step - k < tiles:
                stage(step - k)
    for cp in started:
        cp.wait_send()
    theirs.wait_send()


def core_stage(queries, keys, values, outw, student, teacher, gain, cosines, sines, loss_scale, score_scale, collective_id):
    rows, cols = queries.shape
    width = student.shape[1]
    share = width // 4
    wide = -(-share // 128) * 128
    tiles = rows // TILE
    f32, bf16 = jnp.float32, jnp.bfloat16

    def body(*refs):
        core_kernel(loss_scale, score_scale, float(width), *refs)

    vmem, anywhere = pl.BlockSpec(memory_space=pltpu.VMEM), pl.BlockSpec(memory_space=pl.ANY)
    return pl.pallas_call(
        body,
        out_shape=[
            jax.ShapeDtypeStruct((rows, share), bf16),
            jax.ShapeDtypeStruct((rows, share), bf16),
            jax.ShapeDtypeStruct((4, rows, cols), bf16),
            jax.ShapeDtypeStruct((rows, cols), bf16),
        ],
        in_specs=[vmem] * 4 + [anywhere] * 2 + [vmem] * 3,
        out_specs=[vmem] * 4,
        scratch_shapes=[
            pltpu.VMEM((rows, share), f32),
            pltpu.VMEM((tiles, 2 * TILE, W + TILE), f32),
            pltpu.VMEM((4, rows, cols), bf16),
            pltpu.VMEM((3, rows, cols), bf16),
            pltpu.VMEM((rows, wide), bf16),
            pltpu.VMEM((rows, wide), bf16),
            pltpu.VMEM((2, 8, rows), f32),
            pltpu.VMEM((2, 3, 8, rows), f32),
            pltpu.SemaphoreType.DMA((tiles, 14)),
            pltpu.SemaphoreType.DMA((tiles, 14)),
            pltpu.SemaphoreType.DMA((3,)),
        ],
        compiler_params=pltpu.CompilerParams(
            collective_id=collective_id, has_side_effects=True, vmem_limit_bytes=VMEM_CAP
        ),
        name="core_stage",
    )(queries, keys, values, outw, student, teacher, gain, cosines, sines)


def from_behind(x, axis, by):
    count = lax.axis_size(axis)
    pairs = [(i, i + by) for i in range(count) if 0 <= i + by < count]
    return lax.ppermute(x, axis, pairs)


def swap_share(block):
    route = []
    for sec in range(2):
        for dp in range(16):
            for t in range(4):
                high, low = dp // 8, dp % 8
                there = ((t // 2) * 16 + (t % 2) * 8 + low) * 4 + sec * 2 + high
                route.append(((sec * 16 + dp) * 4 + t, there))
    return lax.ppermute(block, ("sec", "dp", "tensor"), route)


def rotate(values, cos_table, sin_table, sign_value):
    row_count = values.shape[0]
    half_dim = cos_table.shape[1]
    per_head = values.reshape(row_count, -1, 2 * half_dim)
    leading = per_head[:, :, :half_dim]
    trailing = per_head[:, :, half_dim:]
    cosines = cos_table[:, None, :]
    sin_scaled = sign_value * sin_table[:, None, :]
    rotated = jnp.concatenate(
        [leading * cosines - trailing * sin_scaled, trailing * cosines + leading * sin_scaled],
        axis=2,
    )
    return rotated.reshape(row_count, -1)


def shards(
    student_rows,
    teacher_rows,
    norm_gain,
    post_gain,
    query_weight,
    key_weight,
    value_weight,
    out_weight,
):
    f32, bf16 = jnp.float32, jnp.bfloat16
    tok_count = student_rows.shape[1]
    model_width = student_rows.shape[2]
    tensor_count = lax.axis_size("tensor")
    share_cols = model_width // tensor_count
    data_count = lax.axis_size("sec") * lax.axis_size("dp")
    blocks_back = (W + tok_count - 1) // tok_count
    query_cols = query_weight.shape[1]
    kv_cols = key_weight.shape[1]
    score_scale = 1.0 / math.sqrt(HD)
    loss_scale = 2.0 / math.sqrt(data_count * tok_count)
    out_block = swap_share(out_weight)
    key_value = jnp.concatenate([key_weight, value_weight], axis=1)
    items = ((0, 0, 512, True), (1, 0, 512, False), (2, 0, 256, True), (2, 256, 256, False))
    query_full, kv_full, out_share = plane_gather((query_weight, key_value, out_block), items, 0)
    query_full = query_full.reshape(model_width, query_cols)
    kv_full = kv_full.reshape(model_width, 2 * kv_cols)
    out_share = out_share.reshape(tensor_count, share_cols, query_cols)

    student_f = student_rows[0].astype(f32)
    inverse = lax.rsqrt(jnp.mean(student_f * student_f, axis=1, keepdims=True) + norm_eps)
    normed = (student_f * inverse * norm_gain).astype(bf16)
    first_pos = lax.axis_index("dp") * tok_count
    half_dim = HD // 2
    inv_freq = jnp.power(f32(rope_base), -2.0 * jnp.arange(half_dim, dtype=f32) / HD)
    positions = (first_pos + jnp.arange(tok_count, dtype=jnp.int32)).astype(f32)
    angles = positions[:, None] * inv_freq[None, :]
    cos_table = jnp.cos(angles)
    sin_table = jnp.sin(angles)
    key_values = jnp.dot(normed, kv_full, preferred_element_type=f32)
    key_rows = rotate(key_values[:, :kv_cols], cos_table, sin_table, 1.0).astype(bf16)
    value_rows = key_values[:, kv_cols:].astype(bf16)
    key_parts = [key_rows]
    value_parts = [value_rows]
    for offset in range(1, blocks_back + 1):
        earlier_keys, earlier_values = from_behind((key_rows, value_rows), "dp", offset)
        key_parts = [earlier_keys] + key_parts
        value_parts = [earlier_values] + value_parts
    queries = rotate(
        jnp.dot(normed, query_full, preferred_element_type=f32), cos_table, sin_table, 1.0
    ).astype(bf16)
    key_window = jnp.concatenate(key_parts, axis=0)
    value_window = jnp.concatenate(value_parts, axis=0)
    layer_share, pre_share, mixed_all, query_pre = core_stage(
        queries, key_window, value_window, out_share, student_rows[0], teacher_rows[0], post_gain[None],
        cos_table, sin_table, loss_scale, score_scale, 1,
    )
    query_term = jnp.einsum("td,te->de", normed, query_pre, preferred_element_type=f32).astype(bf16)
    out_term = jnp.einsum("td,ate->ade", pre_share, mixed_all, preferred_element_type=f32).astype(bf16)
    query_grad, out_grad = plane_scatter(
        (query_term.reshape(32, -1, query_cols), out_term.reshape(32, -1, query_cols)), (f32, bf16), 2
    )
    return (layer_share[None], query_grad, swap_share(out_grad).astype(f32))


def solution(mesh):
    in_specs = (
        P("sec", "dp", None),
        P("sec", "dp", None),
        P(),
        P(),
        P(("sec", "dp"), "tensor"),
        P(("sec", "dp"), "tensor"),
        P(("sec", "dp"), "tensor"),
        P(("sec", "dp"), "tensor"),
    )
    out_specs = (P("sec", "dp", "tensor"), P(("sec", "dp"), "tensor"), P(("sec", "dp"), "tensor"))
    return jax.shard_map(shards, mesh=mesh, in_specs=in_specs, out_specs=out_specs, check_vma=False)
```
